32 devices in a mesh: range: 4 (over z), doppler: 8 (over y, x, core).
Axes of the slice: x: 2, y: 2, z: 4, core: 2. Of those that a mesh axis runs over, the one named last changes fastest.
Arguments:
- snapshot: bfloat16 [2, 2048, 2, 64, 128], P(None, ('range', 'doppler')), may hold values from -120 to 120
- spatial: bfloat16 [2, 128, 2, 128], replicated, may hold values from -0.375 to 0.375
- tap_weights: float32 [64, 2, 3, 128], P('doppler'), may hold values from -6 to 6
- step_size: float32 [64], P('doppler'), may hold values from 0.2 to 0.8
- train_mask: int32 [2, 2048], P(None, 'range'), may hold values 0 or 1
- guard_center: int32 [2], replicated, may hold values from 0 to 2047
Outputs:
- errors: float32 [2, 2, 64, 2048], P(None, None, 'doppler', 'range')
- final_taps: float32 [64, 2, 3, 128], P('doppler')
The draws below stay inside these ranges and needn't reach their ends.
All inputs are finite; a program needn't handle non-finite values. No bound on the sum of `train_mask` on one device may be relied on, other than what follows from the above.
Results may differ from the reference program's by a relative error of at most 0.0057.
Values may be sent and summed in bfloat16 or wider, within the bound.
A program may use at most 64 MiB of HBM per device.

```python
import math
import jax
import jax.numpy as jnp
from jax import lax

CHANNELS = 128
BEAMS = 128
PULSES = 64
TAPS = 3
BLOCKS = 2
GATES = 2048
GUARD = 256


def draw_snapshot(key, part):
    subkeys = jax.random.split(key, 3)
    full_shape = (BLOCKS, GATES, 2, PULSES, CHANNELS)
    gate_fraction = jnp.arange(GATES, dtype=jnp.float32) / GATES
    noise = jax.random.truncated_normal(subkeys[0], -6.0, 6.0, full_shape, jnp.float32)
    rising = jnp.exp(gate_fraction * math.log(3.0))
    gate_gain = jnp.exp(jax.random.uniform(subkeys[1], (BLOCKS, GATES), jnp.float32) * math.log(3.0)) * rising
    channel_gain = jnp.exp(jax.random.uniform(subkeys[2], (CHANNELS,), jnp.float32) * math.log(3.5))
    values = noise * gate_gain[:, :, None, None, None] * channel_gain / 4.0
    return values.astype(jnp.bfloat16)


def set_ends(drawn, own_key, smallest, high):
    spot = [jax.random.randint(jax.random.fold_in(own_key, axis), (), 0, length) for axis, length in enumerate(drawn.shape)]
    longest = drawn.shape.index(max(drawn.shape))
    next_to = spot[:longest] + [(spot[longest] + 1) % drawn.shape[longest]] + spot[longest + 1:]
    return drawn.at[tuple(spot)].set(smallest).at[tuple(next_to)].set(high)


def level_of(key, extent, cuts, low, largest):
    def one(axis_at, shards_of):
        draws = jax.random.uniform(jax.random.fold_in(jax.random.fold_in(key, 6), axis_at), (shards_of,), jnp.float32, low / len(cuts), largest / len(cuts))
        return jnp.repeat(jnp.exp(draws), extent[axis_at] // shards_of).reshape((-1,) + (1,) * (len(extent) - axis_at - 1))

    gain = one(*cuts[0])
    for cut in cuts[1:]:
        gain = gain * one(*cut)
    return gain


def scatter_about(own_key, extent, width, most, cuts=(), kind=jnp.bfloat16):
    loudness = level_of(own_key, extent, cuts, -0.22, 0.18) if cuts else 1.0
    result = jax.random.normal(own_key, extent, jnp.float32) * width * loudness
    return jnp.minimum(jnp.maximum(result, -most), most).astype(kind)


def setup_inputs(seed: int = 0) -> dict:
    streams_of = jax.random.split(jax.random.key(seed), 7)
    snapshot = draw_snapshot(jax.random.fold_in(streams_of[6], 71), 0)
    spatial = scatter_about(streams_of[1], (2, CHANNELS, 2, BEAMS), (2 * CHANNELS) ** -0.5, 0.375)
    tap_weights = scatter_about(streams_of[2], (PULSES, 2, TAPS, BEAMS), 1.0, 6.0, ((0, 8),), jnp.float32)
    step_size = jnp.clip(jnp.exp(math.log(0.8) - 1.3862944 * jax.random.uniform(streams_of[3], (PULSES,), jnp.float32) ** level_of(streams_of[3], (PULSES,), ((0, 8),), -0.2, 0.2)), 0.2, 0.8)
    train_mask = set_ends((jax.random.randint(streams_of[4], (BLOCKS, GATES), 0, 2) < 1).astype(jnp.int32), jax.random.fold_in(streams_of[4], 1), 0, 1)
    guard_center = jax.random.randint(streams_of[5], (BLOCKS,), 0, GATES).astype(jnp.int32)
    return dict(snapshot=snapshot, spatial=spatial, tap_weights=tap_weights, step_size=step_size, train_mask=train_mask, guard_center=guard_center)


def rounded(values):
    return lax.optimization_barrier(values.astype(jnp.bfloat16)).astype(jnp.float32)

def dft_table(pulse_count):
    sample_index = jnp.arange(pulse_count, dtype=jnp.int32)
    phase_index = sample_index[:, None] * sample_index[None, :] % pulse_count
    angles = phase_index.astype(jnp.float32) * (2.0 * math.pi / pulse_count)
    cosine = jnp.cos(angles) / math.sqrt(pulse_count)
    sine_part = jnp.sin(angles) / math.sqrt(pulse_count)
    upper_rows = jnp.stack([cosine, -sine_part], axis=1)
    lower_rows = jnp.stack([sine_part, cosine], axis=1)
    return jnp.stack([upper_rows, lower_rows], axis=0)

def tap_terms(extended):
    bin_width = extended.shape[2] - 2
    auxiliary = jnp.stack([extended[:, :, offset:offset + bin_width] for offset in range(3)], axis=3)
    beam_index = jnp.arange(auxiliary.shape[4], dtype=jnp.int32)
    tap_index = jnp.arange(3, dtype=jnp.int32)
    live_slots = jnp.logical_or(tap_index[:, None] != 1, beam_index[None, :] != 0)
    auxiliary = jnp.where(live_slots, auxiliary, jnp.zeros_like(auxiliary))
    main_beam = extended[:, :, 1:1 + bin_width, 0]
    return (auxiliary, main_beam)

def canceller(extended, weights, trained):
    auxiliary, main_beam = tap_terms(extended)
    scaling = 1.0 / math.sqrt(3 * auxiliary.shape[4])
    filtered = jnp.einsum('rskjb,kqjb->rskq', auxiliary, weights)
    real_part = filtered[:, 0, :, 0] + filtered[:, 1, :, 1]
    imag_part = filtered[:, 1, :, 0] - filtered[:, 0, :, 1]
    errors = jnp.stack([main_beam[:, 0] - scaling * real_part, main_beam[:, 1] - scaling * imag_part], axis=1)
    weighted = rounded(errors) * trained[:, None, None]
    cross_sum = jnp.einsum('rqk,rskjb->kqsjb', weighted, auxiliary)
    gradient = jnp.stack([cross_sum[:, 0, 0] + cross_sum[:, 1, 1], cross_sum[:, 0, 1] - cross_sum[:, 1, 0]], axis=1)
    energy = jnp.einsum('rskjb,rskjb->rk', auxiliary, auxiliary)
    power_sum = jnp.einsum('r,rk->k', trained, energy)
    return (errors, gradient, power_sum)

def advance(current, steps, gradient, power_sum):
    slot_count = 3 * current.shape[3]
    normalizer = power_sum / slot_count + 1e-06
    factor = steps * math.sqrt(slot_count) / normalizer
    return current + factor[:, None, None, None] * gradient

def reference(snapshot, spatial, tap_weights, step_size, train_mask, guard_center):
    transform = rounded(dft_table(PULSES))
    spatial_wide = spatial.astype(jnp.float32)
    group_size = math.gcd(GATES, 1024)
    group_count = GATES // group_size
    positions = jnp.arange(GATES, dtype=jnp.int32)
    current = tap_weights
    outputs = []
    for block_index in range(BLOCKS):
        weights = rounded(current)
        outside = jnp.abs(positions - guard_center[block_index]) > GUARD
        trained = jnp.where(outside, train_mask[block_index], 0).astype(jnp.float32)

        def one_group(pieces):
            samples, train_rows = pieces
            beam_data = rounded(jnp.einsum('grpc,rcsb->gspb', samples.astype(jnp.float32), spatial_wide))
            spectra = rounded(jnp.einsum('gspb,sptk->gtkb', beam_data, transform))
            extended = jnp.concatenate([spectra[:, :, -1:], spectra, spectra[:, :, :1]], axis=2)
            return canceller(extended, weights, train_rows)
        errors, gradient, power_sum = lax.map(one_group, (snapshot[block_index].reshape(group_count, group_size, 2, PULSES, CHANNELS), trained.reshape(group_count, group_size)))
        outputs.append(jnp.transpose(errors, (2, 3, 0, 1)).reshape(2, PULSES, GATES))
        current = advance(current, step_size, lax.optimization_barrier(jnp.sum(gradient, axis=0)), lax.optimization_barrier(jnp.sum(power_sum, axis=0)))
    return (jnp.stack(outputs), current)
```

```python
import functools
import math

import jax
import jax.numpy as jnp
import numpy as np
from jax import lax
from jax.experimental import pallas as pl
from jax.experimental.pallas import tpu as pltpu
from jax.sharding import PartitionSpec as P

MESH = pl.DeviceIdType.MESH
F32 = jnp.float32
BF16 = jnp.bfloat16


def dft_matrix(pulses):
    index = np.arange(pulses)
    angles = (index[:, None] * index[None, :] % pulses) * (2.0 * math.pi / pulses)
    cosine = np.cos(angles) / math.sqrt(pulses)
    sine = np.sin(angles) / math.sqrt(pulses)
    upper = np.concatenate([cosine.T, sine.T], axis=1)
    lower = np.concatenate([-sine.T, cosine.T], axis=1)
    return jnp.asarray(np.concatenate([upper, lower], axis=0), dtype=BF16)


def kernel(
    dims,
    snap_ref, spatial_ref, dft_ref, taps_ref, step_ref, trained_ref,
    err_out, taps_out,
    xbuf, spec, specb, trcol, wpad, fpad, epad, rpad, ppad,
    cur, wbuf, wrx, ebuf, erx, gf, gbuf, arx, bbuf, brx,
    x_sem, ag_send, ag_recv, er_send, er_recv, a_send, a_recv, b_send, b_recv,
):
    blocks, gates, pulses, chans, beams, dcount, rcount, chunk = dims
    nb = pulses // dcount
    lanes = 2 * gates
    nchunk = gates // chunk
    taps = 3
    slots = taps * beams
    me = lax.axis_index("doppler")
    mz = lax.axis_index("range")

    def x_copy(l, c):
        part = pl.ds(c * chunk, chunk)
        return pltpu.make_async_copy(snap_ref.at[l, part], xbuf.at[l, part], x_sem.at[l, c])

    for l in range(blocks):
        for c in range(nchunk):
            x_copy(l, c).start()

    barrier = pltpu.get_barrier_semaphore()
    for o in range(1, dcount):
        pl.semaphore_signal(barrier, inc=1, device_id={"doppler": lax.rem(me + o, dcount)}, device_id_type=MESH)
    for o in range(1, rcount):
        pl.semaphore_signal(barrier, inc=1, device_id={"range": lax.rem(mz + o, rcount)}, device_id_type=MESH)

    lane = lax.broadcasted_iota(jnp.int32, (1, lanes), 1)
    sign = jnp.where(lane < gates, 1.0, -1.0).astype(F32)
    blane = lax.broadcasted_iota(jnp.int32, (1, beams), 1)

    for j in range(taps):
        for q in range(2):
            cur[pl.ds((2 * j + q) * nb, nb), :] = taps_ref[:, q, j, :]

    def put_taps(l):
        wbuf[l, 0:6 * nb] = cur[...].astype(BF16)
        wrx[l, me, 0:6 * nb] = cur[...].astype(BF16)

    put_taps(0)
    gf[...] = jnp.zeros_like(gf)
    epad[...] = jnp.zeros_like(epad)
    rows8 = lax.broadcasted_iota(jnp.int32, (8, beams), 0)
    lane8 = lax.broadcasted_iota(jnp.int32, (8, beams), 1)
    pick = jnp.where((rows8 == 6) & (lane8 == 0), 1.0, 0.0).astype(F32)

    def init_w(m, carry):
        wpad[pl.ds(m * 8, 8), :] = pick
        return carry

    lax.fori_loop(0, pulses + 2, init_w, 0)

    pl.semaphore_wait(barrier, dcount - 1 + rcount - 1)

    def ag_copy(l, o):
        return pltpu.make_async_remote_copy(
            src_ref=wbuf.at[l], dst_ref=wrx.at[l, me],
            send_sem=ag_send.at[l, o], recv_sem=ag_recv.at[l, o],
            device_id={"doppler": lax.rem(me + o, dcount)}, device_id_type=MESH)

    def er_copy(l, o):
        peer = lax.rem(me + o, dcount)
        return pltpu.make_async_remote_copy(
            src_ref=ebuf.at[l, peer], dst_ref=erx.at[l, me],
            send_sem=er_send.at[l, o], recv_sem=er_recv.at[l, o],
            device_id={"doppler": peer}, device_id_type=MESH)

    def a_copy(l, o):
        peer = lax.rem(me + o, dcount)
        return pltpu.make_async_remote_copy(
            src_ref=gbuf.at[l, peer], dst_ref=arx.at[l, me],
            send_sem=a_send.at[l, o], recv_sem=a_recv.at[l, o],
            device_id={"doppler": peer}, device_id_type=MESH)

    def b_copy(l, o):
        return pltpu.make_async_remote_copy(
            src_ref=bbuf.at[l], dst_ref=brx.at[l, mz],
            send_sem=b_send.at[l, o], recv_sem=b_recv.at[l, o],
            device_id={"range": lax.rem(mz + o, rcount)}, device_id_type=MESH)

    def spectra(l, first, last):
        def step(c, carry):
            x_copy(l, c).wait()
            x = xbuf[l, pl.ds(c * chunk, chunk)]
            lhs = jnp.concatenate(
                [x[:, 0].reshape(chunk * pulses, chans), x[:, 1].reshape(chunk * pulses, chans)], axis=1)
            y = jnp.dot(lhs, spatial_ref[...], preferred_element_type=F32).astype(BF16)
            cols = []
            for g in range(chunk):
                one = y[g * pulses:(g + 1) * pulses]
                cols.append(jnp.concatenate([one[:, :beams], one[:, beams:]], axis=0))
            o = jnp.dot(dft_ref[...], jnp.concatenate(cols, axis=1), preferred_element_type=F32)
            for g in range(chunk):
                for t in range(2):
                    spec[pl.ds(t * gates + c * chunk + g, pulses, stride=lanes), :] = (
                        o[t * pulses:(t + 1) * pulses, g * beams:(g + 1) * beams])
            return carry

        lax.fori_loop(first, last, step, 0)

    def pack(l):
        row = trained_ref[pl.ds(l, 1), :]
        trcol[...] = jnp.transpose(jnp.broadcast_to(row, (lanes, lanes)))[:, :1] * jnp.ones((1, beams), F32)

        def step(m, carry):
            s = spec[pl.ds(m * lanes, lanes), :].astype(BF16)
            specb[m] = s
            wide = s.astype(F32)
            sq = wide * wide * trcol[...]
            ppad[pl.ds((m + 1) * 8, 8), :] = jnp.sum(sq.reshape(lanes // 8, 8, beams), axis=0)
            return carry

        lax.fori_loop(0, pulses, step, 0, unroll=4)
        ppad[0:8] = ppad[pulses * 8:pulses * 8 + 8]
        ppad[(pulses + 1) * 8:(pulses + 2) * 8] = ppad[8:16]

    def build_w(l):
        for d in range(dcount):
            part = wrx[l, d].astype(F32)
            for j in range(taps):
                for q in range(2):
                    r = 2 * j + q
                    val = part[r * nb:(r + 1) * nb]
                    if j == 1:
                        val = jnp.where(blane == 0, 0.0, val)
                    wpad[pl.ds((d * nb + j) * 8 + r, nb, stride=8), :] = val
        wrap(wpad)

    def wrap(ref):
        ref[pulses * 8:pulses * 8 + 2] = ref[0:2]
        ref[12:14] = ref[(pulses + 1) * 8 + 4:(pulses + 1) * 8 + 6]

    def errors(l):
        def step(m, carry):
            w = wpad[pl.ds((m + 1) * 8, 8), :].astype(BF16)
            fpad[pl.ds((m + 1) * 8, 8), :] = lax.dot_general(
                w, specb[m], (((1,), (1,)), ((), ())), preferred_element_type=F32)
            return carry

        lax.fori_loop(0, pulses, step, 0, unroll=8)
        fpad[0:8] = fpad[pulses * 8:pulses * 8 + 8]
        fpad[(pulses + 1) * 8:(pulses + 2) * 8] = fpad[8:16]
        total = jnp.zeros((pulses, lanes), F32)
        for j in range(taps):
            f0 = fpad[pl.ds(j * 8 + 2 * j, pulses, stride=8), :]
            f1 = fpad[pl.ds(j * 8 + 2 * j + 1, pulses, stride=8), :]
            total = total + f0 + sign * pltpu.roll(f1, gates, 1)
        main = fpad[pl.ds(8 + 6, pulses, stride=8), :]
        err = main - (1.0 / math.sqrt(slots)) * total
        for d in range(dcount):
            ebuf[l, d] = err[d * nb:(d + 1) * nb]
        erx[l, me] = ebuf[l, me]
        for o in range(1, dcount):
            er_copy(l, o).start()
        e0 = err.astype(BF16).astype(F32) * trained_ref[pl.ds(l, 1), :]
        e1 = -sign * pltpu.roll(e0, gates, 1)
        for j in range(taps):
            epad[pl.ds(j * 8 + 2 * j, pulses, stride=8), :] = e0
            epad[pl.ds(j * 8 + 2 * j + 1, pulses, stride=8), :] = e1
        wrap(epad)

    def gradient(l):
        def step(m, carry):
            e = epad[pl.ds((m + 1) * 8, 8), :].astype(BF16)
            rpad[pl.ds((m + 1) * 8, 8), :] = jnp.dot(e, specb[m], preferred_element_type=F32)
            return carry

        lax.fori_loop(0, pulses, step, 0, unroll=8)
        rpad[0:8] = rpad[pulses * 8:pulses * 8 + 8]
        rpad[(pulses + 1) * 8:(pulses + 2) * 8] = rpad[8:16]
        for j in range(taps):
            for q in range(2):
                r = 2 * j + q
                val = rpad[pl.ds(j * 8 + r, pulses, stride=8), :]
                if j == 1:
                    val = jnp.where(blane == 0, 0.0, val)
                for d in range(dcount):
                    gf[d, r * nb:(r + 1) * nb] = val[d * nb:(d + 1) * nb]
        power = jnp.zeros((pulses, beams), F32)
        for j in range(taps):
            one = jnp.zeros((pulses, beams), F32)
            for i in range(8):
                one = one + ppad[pl.ds(j * 8 + i, pulses, stride=8), :]
            if j == 1:
                one = jnp.where(blane == 0, 0.0, one)
            power = power + one
        for d in range(dcount):
            gf[d, 6 * nb:7 * nb] = power[d * nb:(d + 1) * nb]
        gbuf[l] = gf[...].astype(BF16)
        for o in range(1, dcount):
            a_copy(l, o).start()

    def reduce_a(l):
        total = gf[me]
        for o in range(1, dcount):
            a_copy(l, o).wait_recv()
            total = total + arx[l, lax.rem(me + dcount - o, dcount)].astype(F32)
        narrow = total.astype(BF16)
        bbuf[l] = narrow
        brx[l, mz] = narrow
        for o in range(1, rcount):
            b_copy(l, o).start()

    def reduce_b(l):
        for o in range(1, rcount):
            b_copy(l, o).wait_recv()
        total = brx[l, 0].astype(F32)
        for z in range(1, rcount):
            total = total + brx[l, z].astype(F32)
        power = jnp.sum(total[6 * nb:7 * nb], axis=1, keepdims=True)
        rows = lax.broadcasted_iota(jnp.int32, (nb, 1), 0)
        steps = jnp.zeros((nb, 1), F32)
        for i in range(nb):
            steps = jnp.where(rows == i, step_ref[i], steps)
        factor = steps * math.sqrt(slots) / (power / slots + 1e-06)
        for r in range(6):
            part = pl.ds(r * nb, nb)
            cur[part, :] = cur[part, :] + factor * total[r * nb:(r + 1) * nb]

    def send_taps(l):
        for o in range(1, dcount):
            ag_copy(l, o).start()

    def await_taps(l):
        for o in range(1, dcount):
            ag_copy(l, o).wait_recv()
        build_w(l)

    send_taps(0)
    spectra(0, 0, nchunk)
    pack(0)
    await_taps(0)
    for l in range(blocks):
        errors(l)
        gradient(l)
        if l + 1 < blocks:
            spectra(l + 1, 0, nchunk // 2)
            reduce_a(l)
            spectra(l + 1, nchunk // 2, nchunk)
            reduce_b(l)
            put_taps(l + 1)
            send_taps(l + 1)
            pack(l + 1)
            await_taps(l + 1)
        else:
            for k in range(blocks):
                for o in range(1, dcount):
                    er_copy(k, o).wait_recv()
                for i in range(dcount // 2):
                    low = erx[k, 2 * i]
                    high = erx[k, 2 * i + 1]
                    part = pl.ds(i * lanes, lanes)
                    err_out[k, 0, :, part] = jnp.where(lane < gates, low, pltpu.roll(high, gates, 1))
                    err_out[k, 1, :, part] = jnp.where(lane < gates, pltpu.roll(low, gates, 1), high)
            reduce_a(l)
            reduce_b(l)
    for j in range(taps):
        for q in range(2):
            taps_out[:, q, j, :] = cur[pl.ds((2 * j + q) * nb, nb), :]
    for l in range(blocks):
        for o in range(1, dcount):
            ag_copy(l, o).wait_send()
            er_copy(l, o).wait_send()
            a_copy(l, o).wait_send()
        for o in range(1, rcount):
            b_copy(l, o).wait_send()


def body(snapshot, spatial, tap_weights, step_size, train_mask, guard_center):
    blocks, gates, _, pulses, chans = snapshot.shape
    beams = spatial.shape[3]
    rcount = lax.axis_size("range")
    dcount = lax.axis_size("doppler")
    nb = pulses // dcount
    lanes = 2 * gates
    chunk = math.gcd(gates, 8)
    nchunk = gates // chunk
    guard_width = gates * rcount * dcount // 8
    start = lax.axis_index("doppler") * gates
    mine = lax.dynamic_slice_in_dim(train_mask, start, gates, axis=1)
    positions = lax.axis_index("range") * (gates * dcount) + start + jnp.arange(gates, dtype=jnp.int32)
    outside = jnp.abs(positions[None, :] - guard_center[:, None]) > guard_width
    trained = jnp.where(outside, mine, 0).astype(F32)
    trained = jnp.concatenate([trained, trained], axis=1)
    wrows = -(-6 * nb // 16) * 16
    dims = (blocks, gates, pulses, chans, beams, dcount, rcount, chunk)
    vmem = pl.BlockSpec(memory_space=pltpu.VMEM)
    dma = pltpu.SemaphoreType.DMA
    pad = (pulses + 2) * 8
    return pl.pallas_call(
        functools.partial(kernel, dims),
        out_shape=(
            jax.ShapeDtypeStruct((blocks, 2, nb, gates * dcount), F32),
            jax.ShapeDtypeStruct((nb, 2, 3, beams), F32),
        ),
        in_specs=[
            pl.BlockSpec(memory_space=pl.ANY), vmem, vmem, vmem,
            pl.BlockSpec(memory_space=pltpu.SMEM), vmem,
        ],
        out_specs=(vmem, vmem),
        scratch_shapes=[
            pltpu.VMEM((blocks, gates, 2, pulses, chans), BF16),
            pltpu.VMEM((pulses * lanes, beams), F32),
            pltpu.VMEM((pulses, lanes, beams), BF16),
            pltpu.VMEM((lanes, beams), F32),
            pltpu.VMEM((pad, beams), F32),
            pltpu.VMEM((pad, lanes), F32),
            pltpu.VMEM((pad, lanes), F32),
            pltpu.VMEM((pad, beams), F32),
            pltpu.VMEM((pad, beams), F32),
            pltpu.VMEM((6 * nb, beams), F32),
            pltpu.VMEM((blocks, wrows, beams), BF16),
            pltpu.VMEM((blocks, dcount, wrows, beams), BF16),
            pltpu.VMEM((blocks, dcount, nb, lanes), F32),
            pltpu.VMEM((blocks, dcount, nb, lanes), F32),
            pltpu.VMEM((dcount, 8 * nb, beams), F32),
            pltpu.VMEM((blocks, dcount, 8 * nb, beams), BF16),
            pltpu.VMEM((blocks, dcount, 8 * nb, beams), BF16),
            pltpu.VMEM((blocks, 8 * nb, beams), BF16),
            pltpu.VMEM((blocks, rcount, 8 * nb, beams), BF16),
            dma((blocks, nchunk)),
            dma((blocks, dcount)), dma((blocks, dcount)),
            dma((blocks, dcount)), dma((blocks, dcount)),
            dma((blocks, dcount)), dma((blocks, dcount)),
            dma((blocks, rcount)), dma((blocks, rcount)),
        ],
        compiler_params=pltpu.CompilerParams(collective_id=0, has_side_effects=True),
    )(
        snapshot,
        spatial.reshape(2 * chans, 2 * beams),
        dft_matrix(pulses),
        tap_weights,
        step_size,
        trained,
    )


def solution(mesh):
    return jax.shard_map(
        body,
        mesh=mesh,
        in_specs=(
            P(None, ("range", "doppler"), None, None, None),
            P(),
            P("doppler", None, None, None),
            P("doppler"),
            P(None, "range"),
            P(),
        ),
        out_specs=(P(None, None, "doppler", "range"), P("doppler", None, None, None)),
        check_vma=False,
    )
```

```python
import functools
import math

import jax
import jax.numpy as jnp
import numpy as np
from jax import lax
from jax.experimental import pallas as pl
from jax.experimental.pallas import tpu as pltpu
from jax.sharding import PartitionSpec as P

MESH = pl.DeviceIdType.MESH
F32 = jnp.float32
BF16 = jnp.bfloat16


def dft_matrix(pulses):
    index = np.arange(pulses)
    angles = (index[:, None] * index[None, :] % pulses) * (2.0 * math.pi / pulses)
    cosine = np.cos(angles) / math.sqrt(pulses)
    sine = np.sin(angles) / math.sqrt(pulses)
    upper = np.concatenate([cosine.T, sine.T], axis=1)
    lower = np.concatenate([-sine.T, cosine.T], axis=1)
    return jnp.asarray(np.concatenate([upper, lower], axis=0), dtype=BF16)


def kernel(
    dims,
    snap_ref, spatial_ref, dft_ref, taps_ref, step_ref, mask_ref, guard_ref,
    err_out, taps_out,
    xbuf, spec, trained, wpad, fpad, epad, rpad, smat,
    cur, wbuf, wrx, ebuf, erx, gf, gbuf, arx, bbuf, brx,
    x_sem, ag_send, ag_recv, er_send, er_recv, a_send, a_recv, b_send, b_recv,
):
    blocks, gates, pulses, chans, beams, dcount, rcount, chunk = dims
    nb = pulses // dcount
    lanes = 2 * gates
    pitch = lanes + 8
    nchunk = gates // chunk
    taps = 3
    slots = taps * beams
    me = lax.axis_index("doppler")
    mz = lax.axis_index("range")

    def x_copy(l, c):
        part = pl.ds(c * chunk, chunk)
        return pltpu.make_async_copy(snap_ref.at[l, part], xbuf.at[l, part], x_sem.at[l, c])

    for l in range(blocks):
        for c in range(nchunk):
            x_copy(l, c).start()

    barrier = pltpu.get_barrier_semaphore()
    for o in range(1, dcount):
        pl.semaphore_signal(barrier, inc=1, device_id={"doppler": lax.rem(me + o, dcount)}, device_id_type=MESH)
    for o in range(1, rcount):
        pl.semaphore_signal(barrier, inc=1, device_id={"range": lax.rem(mz + o, rcount)}, device_id_type=MESH)

    lane = lax.broadcasted_iota(jnp.int32, (1, lanes), 1)
    sign = jnp.where(lane < gates, 1.0, -1.0).astype(F32)
    blane = lax.broadcasted_iota(jnp.int32, (1, beams), 1)

    for j in range(taps):
        for q in range(2):
            cur[pl.ds((2 * j + q) * nb, nb), :] = taps_ref[:, j, q, :]

    mask = jnp.zeros((blocks, lanes), jnp.int32)
    for i in range(dcount // 2):
        mask = jnp.where(me // 2 == i, mask_ref[:, i * lanes:(i + 1) * lanes], mask)
    swapped = pltpu.roll(mask, gates, 1)
    even = jnp.where(lane < gates, mask, swapped)
    odd = jnp.where(lane < gates, swapped, mask)
    mask = jnp.where(lax.rem(me, 2) == 0, even, odd)
    position = (mz * dcount + me) * gates + jnp.where(lane < gates, lane, lane - gates)
    guard_width = gates * rcount * dcount // 8
    for l in range(blocks):
        outside = jnp.abs(position - guard_ref[l]) > guard_width
        trained[l:l + 1, :] = jnp.where(outside, mask[l:l + 1], 0).astype(F32)

    for r in range(2):
        for s in range(2):
            smat[r * chans:(r + 1) * chans, s * beams:(s + 1) * beams] = spatial_ref[r, :, s, :]

    def put_taps(l):
        wbuf[l, 0:6 * nb] = cur[...].astype(BF16)
        wrx[l, me, 0:6 * nb] = cur[...].astype(BF16)

    put_taps(0)
    gf[...] = jnp.zeros_like(gf)
    epad[...] = jnp.zeros_like(epad)
    rows8 = lax.broadcasted_iota(jnp.int32, (8, beams), 0)
    lane8 = lax.broadcasted_iota(jnp.int32, (8, beams), 1)
    pick = jnp.where((rows8 == 6) & (lane8 == 0), 1.0, 0.0).astype(F32)

    def init_w(m, carry):
        wpad[pl.ds(m * 8, 8), :] = pick
        return carry

    lax.fori_loop(0, pulses + 2, init_w, 0)

    pl.semaphore_wait(barrier, dcount - 1 + rcount - 1)

    def ag_copy(l, o):
        return pltpu.make_async_remote_copy(
            src_ref=wbuf.at[l], dst_ref=wrx.at[l, me],
            send_sem=ag_send.at[l, o], recv_sem=ag_recv.at[l, o],
            device_id={"doppler": lax.rem(me + o, dcount)}, device_id_type=MESH)

    def er_copy(l, o):
        peer = lax.rem(me + o, dcount)
        return pltpu.make_async_remote_copy(
            src_ref=ebuf.at[l, peer], dst_ref=erx.at[l, me],
            send_sem=er_send.at[l, o], recv_sem=er_recv.at[l, o],
            device_id={"doppler": peer}, device_id_type=MESH)

    def a_copy(l, o):
        peer = lax.rem(me + o, dcount)
        return pltpu.make_async_remote_copy(
            src_ref=gbuf.at[l, peer], dst_ref=arx.at[l, me],
            send_sem=a_send.at[l, o], recv_sem=a_recv.at[l, o],
            device_id={"doppler": peer}, device_id_type=MESH)

    def b_copy(l, o):
        return pltpu.make_async_remote_copy(
            src_ref=bbuf.at[l], dst_ref=brx.at[l, mz],
            send_sem=b_send.at[l, o], recv_sem=b_recv.at[l, o],
            device_id={"range": lax.rem(mz + o, rcount)}, device_id_type=MESH)

    def spectra(l, first, last):
        def step(c, carry):
            x_copy(l, c).wait()
            x = xbuf[l, pl.ds(c * chunk, chunk)]
            lhs = jnp.concatenate(
                [x[:, 0].reshape(chunk * pulses, chans), x[:, 1].reshape(chunk * pulses, chans)], axis=1)
            y = jnp.dot(lhs, smat[...], preferred_element_type=F32).astype(BF16)
            cols = []
            for g in range(chunk):
                one = y[g * pulses:(g + 1) * pulses]
                cols.append(jnp.concatenate([one[:, :beams], one[:, beams:]], axis=0))
            o = jnp.dot(dft_ref[...], jnp.concatenate(cols, axis=1), preferred_element_type=F32)
            for g in range(chunk):
                for t in range(2):
                    spec[pl.ds(t * gates + c * chunk + g, pulses, stride=pitch), :] = (
                        o[t * pulses:(t + 1) * pulses, g * beams:(g + 1) * beams])
            return carry

        lax.fori_loop(first, last, step, 0)

    def bin_spectra(m):
        return spec[pl.ds(pl.multiple_of(m * pitch, 8), lanes), :].astype(BF16)

    def build_w(l):
        for d in range(dcount):
            part = wrx[l, d].astype(F32)
            for j in range(taps):
                for q in range(2):
                    r = 2 * j + q
                    val = part[r * nb:(r + 1) * nb]
                    if j == 1:
                        val = jnp.where(blane == 0, 0.0, val)
                    wpad[pl.ds((d * nb + j) * 8 + r, nb, stride=8), :] = val
        wrap(wpad)

    def wrap(ref):
        ref[pulses * 8:pulses * 8 + 2] = ref[0:2]
        ref[12:14] = ref[(pulses + 1) * 8 + 4:(pulses + 1) * 8 + 6]

    def errors(l):
        def step(i, carry):
            m = 2 * i
            w = wpad[pl.ds(pl.multiple_of((m + 1) * 8, 8), 16), :].astype(BF16)
            pair = jnp.concatenate([bin_spectra(m), bin_spectra(m + 1)], axis=0)
            f = lax.dot_general(w, pair, (((1,), (1,)), ((), ())), preferred_element_type=F32)
            fpad[pl.ds(pl.multiple_of((m + 1) * 8, 8), 8), :] = f[:8, :lanes]
            fpad[pl.ds(pl.multiple_of((m + 2) * 8, 8), 8), :] = f[8:, lanes:]
            return carry

        lax.fori_loop(0, pulses // 2, step, 0, unroll=8)
        fpad[0:8] = fpad[pulses * 8:pulses * 8 + 8]
        fpad[(pulses + 1) * 8:(pulses + 2) * 8] = fpad[8:16]
        total = jnp.zeros((pulses, lanes), F32)
        for j in range(taps):
            f0 = fpad[pl.ds(j * 8 + 2 * j, pulses, stride=8), :]
            f1 = fpad[pl.ds(j * 8 + 2 * j + 1, pulses, stride=8), :]
            total = total + f0 + sign * pltpu.roll(f1, gates, 1)
        main = fpad[pl.ds(8 + 6, pulses, stride=8), :]
        err = main - (1.0 / math.sqrt(slots)) * total
        for d in range(dcount):
            ebuf[l, d] = err[d * nb:(d + 1) * nb]
        erx[l, me] = ebuf[l, me]
        for o in range(1, dcount):
            er_copy(l, o).start()
        e0 = err.astype(BF16).astype(F32) * trained[l:l + 1, :]
        e1 = -sign * pltpu.roll(e0, gates, 1)
        for j in range(taps):
            epad[pl.ds(j * 8 + 2 * j, pulses, stride=8), :] = e0
            epad[pl.ds(j * 8 + 2 * j + 1, pulses, stride=8), :] = e1
        wrap(epad)

    def gradient(l):
        rows = lax.broadcasted_iota(jnp.int32, (8, lanes), 0)
        keep = jnp.where(rows == 6, trained[l:l + 1, :], 0.0).astype(BF16)

        def step(m, carry):
            part = pl.ds(pl.multiple_of((m + 1) * 8, 8), 8)
            e = jnp.concatenate([epad[part, :].astype(BF16), keep], axis=1)
            one = bin_spectra(m)
            both = jnp.concatenate([one, one * one], axis=0)
            rpad[part, :] = jnp.dot(e, both, preferred_element_type=F32)
            return carry

        lax.fori_loop(0, pulses, step, 0, unroll=8)
        rpad[0:8] = rpad[pulses * 8:pulses * 8 + 8]
        rpad[(pulses + 1) * 8:(pulses + 2) * 8] = rpad[8:16]
        for j in range(taps):
            for q in range(2):
                r = 2 * j + q
                val = rpad[pl.ds(j * 8 + r, pulses, stride=8), :]
                if j == 1:
                    val = jnp.where(blane == 0, 0.0, val)
                for d in range(dcount):
                    gf[d, r * nb:(r + 1) * nb] = val[d * nb:(d + 1) * nb]
        power = jnp.zeros((pulses, beams), F32)
        for j in range(taps):
            one = rpad[pl.ds(j * 8 + 6, pulses, stride=8), :]
            if j == 1:
                one = jnp.where(blane == 0, 0.0, one)
            power = power + one
        for d in range(dcount):
            gf[d, 6 * nb:7 * nb] = power[d * nb:(d + 1) * nb]
        gbuf[l] = gf[...].astype(BF16)
        for o in range(1, dcount):
            a_copy(l, o).start()

    def reduce_a(l):
        total = gf[me]
        for o in range(1, dcount):
            a_copy(l, o).wait_recv()
            total = total + arx[l, lax.rem(me + dcount - o, dcount)].astype(F32)
        narrow = total.astype(BF16)
        bbuf[l] = narrow
        brx[l, mz] = narrow
        for o in range(1, rcount):
            b_copy(l, o).start()

    def reduce_b(l):
        for o in range(1, rcount):
            b_copy(l, o).wait_recv()
        total = brx[l, 0].astype(F32)
        for z in range(1, rcount):
            total = total + brx[l, z].astype(F32)
        power = jnp.sum(total[6 * nb:7 * nb], axis=1, keepdims=True)
        rows = lax.broadcasted_iota(jnp.int32, (nb, 1), 0)
        steps = jnp.zeros((nb, 1), F32)
        for i in range(nb):
            steps = jnp.where(rows == i, step_ref[i], steps)
        factor = steps * math.sqrt(slots) / (power / slots + 1e-06)
        for r in range(6):
            part = pl.ds(r * nb, nb)
            cur[part, :] = cur[part, :] + factor * total[r * nb:(r + 1) * nb]

    def send_taps(l):
        for o in range(1, dcount):
            ag_copy(l, o).start()

    def await_taps(l):
        for o in range(1, dcount):
            ag_copy(l, o).wait_recv()
        build_w(l)

    send_taps(0)
    spectra(0, 0, nchunk)
    await_taps(0)
    for l in range(blocks):
        errors(l)
        gradient(l)
        if l + 1 < blocks:
            spectra(l + 1, 0, nchunk // 2)
            reduce_a(l)
            spectra(l + 1, nchunk // 2, nchunk)
            reduce_b(l)
            put_taps(l + 1)
            send_taps(l + 1)
            await_taps(l + 1)
        else:
            for k in range(blocks):
                for o in range(1, dcount):
                    er_copy(k, o).wait_recv()
                for i in range(dcount // 2):
                    low = erx[k, 2 * i]
                    high = erx[k, 2 * i + 1]
                    part = pl.ds(i * lanes, lanes)
                    err_out[k, 0, :, part] = jnp.where(lane < gates, low, pltpu.roll(high, gates, 1))
                    err_out[k, 1, :, part] = jnp.where(lane < gates, pltpu.roll(low, gates, 1), high)
            reduce_a(l)
            reduce_b(l)
    for j in range(taps):
        for q in range(2):
            taps_out[:, j, q, :] = cur[pl.ds((2 * j + q) * nb, nb), :]
    for l in range(blocks):
        for o in range(1, dcount):
            ag_copy(l, o).wait_send()
            er_copy(l, o).wait_send()
            a_copy(l, o).wait_send()
        for o in range(1, rcount):
            b_copy(l, o).wait_send()


def body(snapshot, spatial, tap_weights, step_size, train_mask, guard_center):
    blocks, gates, _, pulses, chans = snapshot.shape
    beams = spatial.shape[3]
    rcount = lax.axis_size("range")
    dcount = lax.axis_size("doppler")
    nb = pulses // dcount
    lanes = 2 * gates
    chunk = math.gcd(gates, 8)
    nchunk = gates // chunk
    wrows = -(-6 * nb // 16) * 16
    dims = (blocks, gates, pulses, chans, beams, dcount, rcount, chunk)
    vmem = pl.BlockSpec(memory_space=pltpu.VMEM)
    dma = pltpu.SemaphoreType.DMA
    pad = (pulses + 2) * 8
    errors, taps = pl.pallas_call(
        functools.partial(kernel, dims),
        out_shape=(
            jax.ShapeDtypeStruct((blocks, 2, nb, gates * dcount), F32),
            jax.ShapeDtypeStruct((nb, 3, 2, beams), F32),
        ),
        in_specs=[
            pl.BlockSpec(memory_space=pl.ANY), vmem, vmem, vmem,
            pl.BlockSpec(memory_space=pltpu.SMEM), vmem, pl.BlockSpec(memory_space=pltpu.SMEM),
        ],
        out_specs=(vmem, vmem),
        scratch_shapes=[
            pltpu.VMEM((blocks, gates, 2, pulses, chans), BF16),
            pltpu.VMEM((pulses * (lanes + 8), beams), F32),
            pltpu.VMEM((blocks, lanes), F32),
            pltpu.VMEM((pad, beams), F32),
            pltpu.VMEM((pad, lanes), F32),
            pltpu.VMEM((pad, lanes), F32),
            pltpu.VMEM((pad, beams), F32),
            pltpu.VMEM((2 * chans, 2 * beams), BF16),
            pltpu.VMEM((6 * nb, beams), F32),
            pltpu.VMEM((blocks, wrows, beams), BF16),
            pltpu.VMEM((blocks, dcount, wrows, beams), BF16),
            pltpu.VMEM((blocks, dcount, nb, lanes), F32),
            pltpu.VMEM((blocks, dcount, nb, lanes), F32),
            pltpu.VMEM((dcount, 8 * nb, beams), F32),
            pltpu.VMEM((blocks, dcount, 8 * nb, beams), BF16),
            pltpu.VMEM((blocks, dcount, 8 * nb, beams), BF16),
            pltpu.VMEM((blocks, 8 * nb, beams), BF16),
            pltpu.VMEM((blocks, rcount, 8 * nb, beams), BF16),
            dma((blocks, nchunk)),
            dma((blocks, dcount)), dma((blocks, dcount)),
            dma((blocks, dcount)), dma((blocks, dcount)),
            dma((blocks, dcount)), dma((blocks, dcount)),
            dma((blocks, rcount)), dma((blocks, rcount)),
        ],
        compiler_params=pltpu.CompilerParams(collective_id=0, has_side_effects=True),
    )(
        snapshot,
        spatial,
        dft_matrix(pulses),
        jnp.transpose(tap_weights, (0, 2, 1, 3)),
        step_size,
        train_mask,
        guard_center,
    )
    return (errors, jnp.transpose(taps, (0, 2, 1, 3)))


def solution(mesh):
    return jax.shard_map(
        body,
        mesh=mesh,
        in_specs=(
            P(None, ("range", "doppler"), None, None, None),
            P(),
            P("doppler", None, None, None),
            P("doppler"),
            P(None, "range"),
            P(),
        ),
        out_specs=(P(None, None, "doppler", "range"), P("doppler", None, None, None)),
        check_vma=False,
    )
```

```python
import functools
import math

import jax
import jax.numpy as jnp
import numpy as np
from jax import lax
from jax.experimental import pallas as pl
from jax.experimental.pallas import tpu as pltpu
from jax.sharding import PartitionSpec as P

MESH = pl.DeviceIdType.MESH
F32 = jnp.float32
BF16 = jnp.bfloat16


def dft_matrix(pulses):
    index = np.arange(pulses)
    angles = (index[:, None] * index[None, :] % pulses) * (2.0 * math.pi / pulses)
    cosine = np.cos(angles) / math.sqrt(pulses)
    sine = np.sin(angles) / math.sqrt(pulses)
    upper = np.concatenate([cosine.T, sine.T], axis=1)
    lower = np.concatenate([-sine.T, cosine.T], axis=1)
    return jnp.asarray(np.concatenate([upper, lower], axis=0), dtype=BF16)


def kernel(
    dims,
    snap_ref, spatial_ref, dft_ref, taps_ref, step_ref, mask_ref, guard_ref,
    err_out, taps_out,
    xbuf, spec, trained, wpad, fpad, epad, rpad, smat,
    cur, wbuf, wrx, ebuf, erx, gf, gbuf, arx, bbuf, brx,
    x_sem, ag_send, ag_recv, er_send, er_recv, a_send, a_recv, b_send, b_recv,
):
    blocks, gates, pulses, chans, beams, dcount, rcount, chunk = dims
    nb = pulses // dcount
    lanes = 2 * gates
    pitch = lanes + 8
    nchunk = gates // chunk
    taps = 3
    slots = taps * beams
    me = lax.axis_index("doppler")
    mz = lax.axis_index("range")

    def x_copy(l, c):
        part = pl.ds(c * chunk, chunk)
        return pltpu.make_async_copy(snap_ref.at[l, part], xbuf.at[l, part], x_sem.at[l, c])

    for l in range(blocks):
        for c in range(nchunk):
            x_copy(l, c).start()

    barrier = pltpu.get_barrier_semaphore()
    for o in range(1, dcount):
        pl.semaphore_signal(barrier, inc=1, device_id={"doppler": lax.rem(me + o, dcount)}, device_id_type=MESH)
    for o in range(1, rcount):
        pl.semaphore_signal(barrier, inc=1, device_id={"range": lax.rem(mz + o, rcount)}, device_id_type=MESH)

    lane = lax.broadcasted_iota(jnp.int32, (1, lanes), 1)
    sign = jnp.where(lane < gates, 1.0, -1.0).astype(F32)
    blane = lax.broadcasted_iota(jnp.int32, (1, beams), 1)

    for j in range(taps):
        for q in range(2):
            cur[pl.ds((2 * j + q) * nb, nb), :] = taps_ref[:, j, q, :]

    mask = jnp.zeros((blocks, lanes), jnp.int32)
    for i in range(dcount // 2):
        mask = jnp.where(me // 2 == i, mask_ref[:, i * lanes:(i + 1) * lanes], mask)
    swapped = pltpu.roll(mask, gates, 1)
    even = jnp.where(lane < gates, mask, swapped)
    odd = jnp.where(lane < gates, swapped, mask)
    mask = jnp.where(lax.rem(me, 2) == 0, even, odd)
    position = (mz * dcount + me) * gates + jnp.where(lane < gates, lane, lane - gates)
    guard_width = gates * rcount * dcount // 8
    for l in range(blocks):
        outside = jnp.abs(position - guard_ref[l]) > guard_width
        trained[l:l + 1, :] = jnp.where(outside, mask[l:l + 1], 0).astype(F32)

    for r in range(2):
        for s in range(2):
            smat[r * chans:(r + 1) * chans, s * beams:(s + 1) * beams] = spatial_ref[r, :, s, :]

    def put_taps(l):
        wbuf[l, 0:6 * nb] = cur[...].astype(BF16)
        wrx[l, me, 0:6 * nb] = cur[...].astype(BF16)

    put_taps(0)
    gf[...] = jnp.zeros_like(gf)
    epad[...] = jnp.zeros_like(epad)
    rows8 = lax.broadcasted_iota(jnp.int32, (8, beams), 0)
    lane8 = lax.broadcasted_iota(jnp.int32, (8, beams), 1)
    pick = jnp.where((rows8 == 6) & (lane8 == 0), 1.0, 0.0).astype(F32)

    def init_w(m, carry):
        wpad[pl.ds(m * 8, 8), :] = pick
        return carry

    lax.fori_loop(0, pulses + 2, init_w, 0)

    def ag_copy(l, o):
        return pltpu.make_async_remote_copy(
            src_ref=wbuf.at[l], dst_ref=wrx.at[l, me],
            send_sem=ag_send.at[l, o], recv_sem=ag_recv.at[l, o],
            device_id={"doppler": lax.rem(me + o, dcount)}, device_id_type=MESH)

    def er_copy(l, o):
        peer = lax.rem(me + o, dcount)
        return pltpu.make_async_remote_copy(
            src_ref=ebuf.at[l, peer], dst_ref=erx.at[l, me],
            send_sem=er_send.at[l, o], recv_sem=er_recv.at[l, o],
            device_id={"doppler": peer}, device_id_type=MESH)

    def a_copy(l, o):
        peer = lax.rem(me + o, dcount)
        return pltpu.make_async_remote_copy(
            src_ref=gbuf.at[l, peer], dst_ref=arx.at[l, me],
            send_sem=a_send.at[l, o], recv_sem=a_recv.at[l, o],
            device_id={"doppler": peer}, device_id_type=MESH)

    def b_copy(l, o):
        return pltpu.make_async_remote_copy(
            src_ref=bbuf.at[l], dst_ref=brx.at[l, mz],
            send_sem=b_send.at[l, o], recv_sem=b_recv.at[l, o],
            device_id={"range": lax.rem(mz + o, rcount)}, device_id_type=MESH)

    def spectra(l, first, last):
        def step(c, carry):
            x_copy(l, c).wait()
            x = xbuf[l, pl.ds(c * chunk, chunk)]
            lhs = jnp.concatenate(
                [x[:, 0].reshape(chunk * pulses, chans), x[:, 1].reshape(chunk * pulses, chans)], axis=1)
            y = jnp.dot(lhs, smat[...], preferred_element_type=F32).astype(BF16)
            cols = []
            for g in range(chunk):
                one = y[g * pulses:(g + 1) * pulses]
                cols.append(jnp.concatenate([one[:, :beams], one[:, beams:]], axis=0))
            o = jnp.dot(dft_ref[...], jnp.concatenate(cols, axis=1), preferred_element_type=F32)
            for g in range(chunk):
                for t in range(2):
                    spec[pl.ds(t * gates + c * chunk + g, pulses, stride=pitch), :] = (
                        o[t * pulses:(t + 1) * pulses, g * beams:(g + 1) * beams])
            return carry

        lax.fori_loop(first, last, step, 0)

    def bin_spectra(m):
        return spec[pl.ds(pl.multiple_of(m * pitch, 8), lanes), :].astype(BF16)

    def build_w(l):
        for d in range(dcount):
            part = wrx[l, d].astype(F32)
            for j in range(taps):
                for q in range(2):
                    r = 2 * j + q
                    val = part[r * nb:(r + 1) * nb]
                    if j == 1:
                        val = jnp.where(blane == 0, 0.0, val)
                    wpad[pl.ds((d * nb + j) * 8 + r, nb, stride=8), :] = val
        wrap(wpad)

    def wrap(ref):
        ref[pulses * 8:pulses * 8 + 2] = ref[0:2]
        ref[12:14] = ref[(pulses + 1) * 8 + 4:(pulses + 1) * 8 + 6]

    def errors(l):
        def step(i, carry):
            m = 2 * i
            w = wpad[pl.ds(pl.multiple_of((m + 1) * 8, 8), 16), :].astype(BF16)
            pair = jnp.concatenate([bin_spectra(m), bin_spectra(m + 1)], axis=0)
            f = lax.dot_general(w, pair, (((1,), (1,)), ((), ())), preferred_element_type=F32)
            fpad[pl.ds(pl.multiple_of((m + 1) * 8, 8), 8), :] = f[:8, :lanes]
            fpad[pl.ds(pl.multiple_of((m + 2) * 8, 8), 8), :] = f[8:, lanes:]
            return carry

        lax.fori_loop(0, pulses // 2, step, 0, unroll=16)
        fpad[0:8] = fpad[pulses * 8:pulses * 8 + 8]
        fpad[(pulses + 1) * 8:(pulses + 2) * 8] = fpad[8:16]
        total = jnp.zeros((pulses, lanes), F32)
        for j in range(taps):
            f0 = fpad[pl.ds(j * 8 + 2 * j, pulses, stride=8), :]
            f1 = fpad[pl.ds(j * 8 + 2 * j + 1, pulses, stride=8), :]
            total = total + f0 + sign * pltpu.roll(f1, gates, 1)
        main = fpad[pl.ds(8 + 6, pulses, stride=8), :]
        err = main - (1.0 / math.sqrt(slots)) * total
        for d in range(dcount):
            ebuf[l, d] = err[d * nb:(d + 1) * nb]
        erx[l, me] = ebuf[l, me]
        for o in range(1, dcount):
            er_copy(l, o).start()
        e0 = err.astype(BF16).astype(F32) * trained[l:l + 1, :]
        e1 = -sign * pltpu.roll(e0, gates, 1)
        for j in range(taps):
            epad[pl.ds(j * 8 + 2 * j, pulses, stride=8), :] = e0
            epad[pl.ds(j * 8 + 2 * j + 1, pulses, stride=8), :] = e1
        wrap(epad)

    def gradient(l):
        rows = lax.broadcasted_iota(jnp.int32, (8, lanes), 0)
        keep = jnp.where(rows == 6, trained[l:l + 1, :], 0.0).astype(BF16)

        def step(m, carry):
            part = pl.ds(pl.multiple_of((m + 1) * 8, 8), 8)
            e = jnp.concatenate([epad[part, :].astype(BF16), keep], axis=1)
            one = bin_spectra(m)
            both = jnp.concatenate([one, one * one], axis=0)
            rpad[part, :] = jnp.dot(e, both, preferred_element_type=F32)
            return carry

        lax.fori_loop(0, pulses, step, 0, unroll=16)
        rpad[0:8] = rpad[pulses * 8:pulses * 8 + 8]
        rpad[(pulses + 1) * 8:(pulses + 2) * 8] = rpad[8:16]
        for j in range(taps):
            for q in range(2):
                r = 2 * j + q
                val = rpad[pl.ds(j * 8 + r, pulses, stride=8), :]
                if j == 1:
                    val = jnp.where(blane == 0, 0.0, val)
                for d in range(dcount):
                    gf[d, r * nb:(r + 1) * nb] = val[d * nb:(d + 1) * nb]
        power = jnp.zeros((pulses, beams), F32)
        for j in range(taps):
            one = rpad[pl.ds(j * 8 + 6, pulses, stride=8), :]
            if j == 1:
                one = jnp.where(blane == 0, 0.0, one)
            power = power + one
        for d in range(dcount):
            gf[d, 6 * nb:7 * nb] = power[d * nb:(d + 1) * nb]
        gbuf[l] = gf[...].astype(BF16)
        for o in range(1, dcount):
            a_copy(l, o).start()

    def reduce_a(l):
        total = gf[me]
        for o in range(1, dcount):
            a_copy(l, o).wait_recv()
            total = total + arx[l, lax.rem(me + dcount - o, dcount)].astype(F32)
        narrow = total.astype(BF16)
        bbuf[l] = narrow
        brx[l, mz] = narrow
        for o in range(1, rcount):
            b_copy(l, o).start()

    def reduce_b(l):
        for o in range(1, rcount):
            b_copy(l, o).wait_recv()
        total = brx[l, 0].astype(F32)
        for z in range(1, rcount):
            total = total + brx[l, z].astype(F32)
        power = jnp.sum(total[6 * nb:7 * nb], axis=1, keepdims=True)
        rows = lax.broadcasted_iota(jnp.int32, (nb, 1), 0)
        steps = jnp.zeros((nb, 1), F32)
        for i in range(nb):
            steps = jnp.where(rows == i, step_ref[i], steps)
        factor = steps * math.sqrt(slots) / (power / slots + 1e-06)
        for r in range(6):
            part = pl.ds(r * nb, nb)
            cur[part, :] = cur[part, :] + factor * total[r * nb:(r + 1) * nb]

    def send_taps(l):
        for o in range(1, dcount):
            ag_copy(l, o).start()

    def await_taps(l):
        for o in range(1, dcount):
            ag_copy(l, o).wait_recv()
        build_w(l)

    early = nchunk // 4
    spectra(0, 0, early)
    pl.semaphore_wait(barrier, dcount - 1 + rcount - 1)
    send_taps(0)
    spectra(0, early, nchunk)
    await_taps(0)
    for l in range(blocks):
        errors(l)
        gradient(l)
        if l + 1 < blocks:
            spectra(l + 1, 0, nchunk // 2)
            reduce_a(l)
            spectra(l + 1, nchunk // 2, nchunk)
            reduce_b(l)
            put_taps(l + 1)
            send_taps(l + 1)
            await_taps(l + 1)
        else:
            for k in range(blocks):
                for o in range(1, dcount):
                    er_copy(k, o).wait_recv()
                for i in range(dcount // 2):
                    low = erx[k, 2 * i]
                    high = erx[k, 2 * i + 1]
                    part = pl.ds(i * lanes, lanes)
                    err_out[k, 0, :, part] = jnp.where(lane < gates, low, pltpu.roll(high, gates, 1))
                    err_out[k, 1, :, part] = jnp.where(lane < gates, pltpu.roll(low, gates, 1), high)
            reduce_a(l)
            reduce_b(l)
    for j in range(taps):
        for q in range(2):
            taps_out[:, j, q, :] = cur[pl.ds((2 * j + q) * nb, nb), :]
    for l in range(blocks):
        for o in range(1, dcount):
            ag_copy(l, o).wait_send()
            er_copy(l, o).wait_send()
            a_copy(l, o).wait_send()
        for o in range(1, rcount):
            b_copy(l, o).wait_send()


def finish(err_ref, taps_ref, err_out, taps_out):
    err_out[...] = err_ref[...]
    taps_out[...] = taps_ref[...]


def body(snapshot, spatial, tap_weights, step_size, train_mask, guard_center):
    blocks, gates, _, pulses, chans = snapshot.shape
    beams = spatial.shape[3]
    rcount = lax.axis_size("range")
    dcount = lax.axis_size("doppler")
    nb = pulses // dcount
    lanes = 2 * gates
    chunk = math.gcd(gates, 16)
    nchunk = gates // chunk
    wrows = -(-6 * nb // 16) * 16
    dims = (blocks, gates, pulses, chans, beams, dcount, rcount, chunk)
    vmem = pl.BlockSpec(memory_space=pltpu.VMEM)
    dma = pltpu.SemaphoreType.DMA
    pad = (pulses + 2) * 8
    errors, taps = pl.pallas_call(
        functools.partial(kernel, dims),
        out_shape=(
            jax.ShapeDtypeStruct((blocks, 2, nb, gates * dcount), F32),
            jax.ShapeDtypeStruct((nb, 3, 2, beams), F32),
        ),
        in_specs=[
            pl.BlockSpec(memory_space=pl.ANY), vmem, vmem, vmem,
            pl.BlockSpec(memory_space=pltpu.SMEM), vmem, pl.BlockSpec(memory_space=pltpu.SMEM),
        ],
        out_specs=(vmem, vmem),
        scratch_shapes=[
            pltpu.VMEM((blocks, gates, 2, pulses, chans), BF16),
            pltpu.VMEM((pulses * (lanes + 8), beams), F32),
            pltpu.VMEM((blocks, lanes), F32),
            pltpu.VMEM((pad, beams), F32),
            pltpu.VMEM((pad, lanes), F32),
            pltpu.VMEM((pad, lanes), F32),
            pltpu.VMEM((pad, beams), F32),
            pltpu.VMEM((2 * chans, 2 * beams), BF16),
            pltpu.VMEM((6 * nb, beams), F32),
            pltpu.VMEM((blocks, wrows, beams), BF16),
            pltpu.VMEM((blocks, dcount, wrows, beams), BF16),
            pltpu.VMEM((blocks, dcount, nb, lanes), F32),
            pltpu.VMEM((blocks, dcount, nb, lanes), F32),
            pltpu.VMEM((dcount, 8 * nb, beams), F32),
            pltpu.VMEM((blocks, dcount, 8 * nb, beams), BF16),
            pltpu.VMEM((blocks, dcount, 8 * nb, beams), BF16),
            pltpu.VMEM((blocks, 8 * nb, beams), BF16),
            pltpu.VMEM((blocks, rcount, 8 * nb, beams), BF16),
            dma((blocks, nchunk)),
            dma((blocks, dcount)), dma((blocks, dcount)),
            dma((blocks, dcount)), dma((blocks, dcount)),
            dma((blocks, dcount)), dma((blocks, dcount)),
            dma((blocks, rcount)), dma((blocks, rcount)),
        ],
        compiler_params=pltpu.CompilerParams(collective_id=0, has_side_effects=True),
    )(
        snapshot,
        spatial,
        dft_matrix(pulses),
        jnp.transpose(tap_weights, (0, 2, 1, 3)),
        step_size,
        train_mask,
        guard_center,
    )
    errors, taps = pl.pallas_call(
        finish,
        out_shape=(
            jax.ShapeDtypeStruct(errors.shape, F32),
            jax.ShapeDtypeStruct(taps.shape, F32),
        ),
        in_specs=[vmem, vmem],
        out_specs=(vmem, vmem),
    )(errors, taps)
    return (errors, jnp.transpose(taps, (0, 2, 1, 3)))


def solution(mesh):
    return jax.shard_map(
        body,
        mesh=mesh,
        in_specs=(
            P(None, ("range", "doppler"), None, None, None),
            P(),
            P("doppler", None, None, None),
            P("doppler"),
            P(None, "range"),
            P(),
        ),
        out_specs=(P(None, None, "doppler", "range"), P("doppler", None, None, None)),
        check_vma=False,
    )
```
